32 devices in a mesh: leaf: 8 (over z, y), row: 2 (over core), col: 2 (over x).
Axes of the slice: x: 2, y: 2, z: 4, core: 2. Of those that a mesh axis runs over, the one named last changes fastest.
Arguments:
- sigma_top: float32 [4096, 4096], P('row', ('leaf', 'col'))
- structure: int32 [8, 16], replicated, may hold values from 0 to 31, as said below
- lower: float32 [8, 2048, 2048], P('leaf', 'row', 'col'), may hold values from -0.25 to 0.25
- dinv: float32 [8, 2048, 2048], P('leaf', 'row', 'col'), may hold values from -6 to 6
Outputs:
- sigma_sj: float32 [8, 2048, 2048], P('leaf', 'row', 'col')
- sigma_jj: float32 [8, 2048, 2048], P('leaf', 'row', 'col')
The draws below stay inside these ranges and needn't reach their ends.
Inputs may be any that keep to these rules, and one draw needn't show every extreme that they name: `structure`: each row lists 16 distinct tiles in increasing order and always holds tile 0 and tile 32 - 1.
All inputs are finite; a program needn't handle non-finite values.
Results may differ from the reference program's by a relative error of at most 0.0003.
Values sent between devices are 32-bit elements; how exact they have to be, the bound alone decides.
No kernel may reach another device: no remote copies, remote signals or barrier semaphores. Data moves between devices by JAX's collectives and lax.ppermute only.
A program may use at most 192 MiB of HBM per device.

```python
import jax
import jax.numpy as jnp
from jax import lax

TILE = 128
R = 4096
W = 2048
NS = 16
S = 2048
CHILDREN = 8


def draw_sigma_top(key, part):
    normal_part = jax.random.normal(key, (R, R), jnp.float32)
    symmetric = 0.5 * (normal_part + normal_part.T)
    second_key = jax.random.fold_in(key, 7)
    diagonal_values = jax.random.uniform(second_key, (R,), jnp.float32, 1.0, 2.0)
    spread = 0.5
    positions = jnp.arange(R)
    on_diagonal = positions[:, None] == positions[None, :]
    off_part = symmetric * (spread / jnp.sqrt(jnp.float32(R)))
    return jnp.where(on_diagonal, diagonal_values[:, None], off_part).astype(jnp.float32)


def draw_structure(key, part):

    def one_child(child):
        child_key = jax.random.fold_in(key, child)
        shuffled = jax.random.permutation(child_key, R // TILE - 2) + 1
        picked = shuffled[:NS - 2]
        ends = jnp.array([0, R // TILE - 1], jnp.int32)
        return jnp.sort(jnp.concatenate([ends, picked.astype(jnp.int32)]))
    return jax.vmap(one_child)(jnp.arange(CHILDREN, dtype=jnp.int32)).astype(jnp.int32)


def steps_of(key, dims, split, low, high):
    factor_of, own = 1.0, jax.random.fold_in(key, 6)
    for axis_at, shards_of in split:
        steps = jnp.exp(jax.random.uniform(jax.random.fold_in(own, axis_at), (shards_of,), jnp.float32, low / len(split), high / len(split)))
        factor_of = factor_of * jnp.repeat(steps, dims[axis_at] // shards_of).reshape([-1 if axis == axis_at else 1 for axis in range(len(dims))])
    return factor_of


def scatter_about(own_key, shape, width, bound, split=(), held_as=jnp.bfloat16):
    level = steps_of(own_key, shape, split, -0.22, 0.18) if split else 1.0
    values = jax.random.normal(own_key, shape, jnp.float32) * width * level
    return jnp.minimum(jnp.maximum(values, -bound), bound).astype(held_as)


def setup_inputs(seed: int = 0) -> dict:
    key_of = jax.random.split(jax.random.key(seed), 5)
    sigma_top = draw_sigma_top(jax.random.fold_in(key_of[4], 71), 0)
    structure = draw_structure(jax.random.fold_in(key_of[4], 71), 0)
    lower = scatter_about(key_of[2], (CHILDREN, S, W), (S // 4) ** -0.5, 0.25, ((0, 8), (1, 2), (2, 2)), jnp.float32)
    dinv = scatter_about(key_of[3], (CHILDREN, W, W), 1.0, 6.0, ((0, 8), (1, 2), (2, 2)), jnp.float32)
    return dict(sigma_top=sigma_top, structure=structure, lower=lower, dinv=dinv)


def reference(sigma_top, structure, lower, dinv):
    within = jnp.arange(TILE, dtype=jnp.int32)

    def one_child(packed):
        tile_list, factor_block, diag_inverse = packed
        indices = (tile_list[:, None] * TILE + within[None, :]).reshape(-1).astype(jnp.int32)
        sigma_ss = jnp.take(jnp.take(sigma_top, indices, axis=0), indices, axis=1)
        cross = -jnp.dot(sigma_ss, factor_block, precision=lax.Precision.HIGHEST, preferred_element_type=jnp.float32)
        front = diag_inverse - jnp.dot(factor_block.T, cross, precision=lax.Precision.HIGHEST, preferred_element_type=jnp.float32)
        return cross, front

    sigma_sj, sigma_jj = lax.map(one_child, (structure, lower, dinv))
    return (sigma_sj, sigma_jj)
```

```python
import jax
import jax.numpy as jnp
from jax import lax
from jax.experimental import pallas as pl
from jax.experimental.pallas import tpu as pltpu
from jax.sharding import Mesh
from jax.sharding import PartitionSpec as P

TILE = 128
HALF = "half"
LOW = "low"


def swap(x, axis, bit):
    size = lax.axis_size(axis)
    return lax.ppermute(x, axis, [(i, i ^ bit) for i in range(size)])


def select_kernel(n_out, per_src, row_core, row_tile, col_half, col_src, col_lane, *refs):
    pieces = refs[:4]
    outs = refs[4 : 4 + n_out]
    table, sems = refs[4 + n_out :]
    copies = [
        pltpu.make_async_copy(pieces[i], table.at[i // 2, i % 2], sems.at[i]) for i in range(4)
    ]
    for copy in copies:
        copy.start()
    for copy in copies:
        copy.wait()
    n_p = outs[0].shape[0]
    n_q = outs[0].shape[2] // TILE
    for child in range(n_out):

        @pl.loop(0, n_p)
        def _(p, child=child):
            core = row_core[child, p]
            tile = row_tile[child, p]
            for q in range(n_q):
                lane = pl.multiple_of(col_lane[child, q], TILE)
                outs[child][p, :, q * TILE : (q + 1) * TILE] = table[
                    core, col_half[child, q], col_src[child, q], tile, :, pl.ds(lane, TILE)
                ]


def select(pieces, rows, cols, row_id, half_id, n_row):
    n_src, rt, k, width = pieces[0].shape
    n_out, n_q = cols.shape
    per_src = width // TILE
    half_cols = n_src * per_src
    tables = (
        (rows // rt) ^ row_id,
        rows % rt,
        (cols // half_cols) ^ half_id,
        cols % half_cols // per_src,
        cols % per_src * TILE,
    )
    n_p = rows.shape[1]
    out = jax.ShapeDtypeStruct((n_p, k, n_q * TILE), jnp.float32)
    return pl.pallas_call(
        lambda *refs: select_kernel(n_out, per_src, *refs),
        out_shape=[out] * n_out,
        grid_spec=pltpu.PrefetchScalarGridSpec(
            num_scalar_prefetch=5,
            grid=(1,),
            in_specs=[pl.BlockSpec(memory_space=pl.ANY)] * 4,
            out_specs=[pl.BlockSpec((n_p, k, n_q * TILE), lambda i, *_: (0, 0, 0))] * n_out,
            scratch_shapes=[
                pltpu.VMEM((2, 2) + pieces[0].shape, jnp.float32),
                pltpu.SemaphoreType.DMA((4,)),
            ],
        ),
        compiler_params=pltpu.CompilerParams(vmem_limit_bytes=32 << 20),
        cost_estimate=pl.CostEstimate(
            flops=0, transcendentals=0, bytes_accessed=2 * 4 * n_out * n_p * k * n_q * TILE
        ),
    )(*tables, *pieces)


def dot(a, b):
    return jnp.dot(a, b, precision=lax.Precision.HIGH, preferred_element_type=jnp.float32)


def body(sigma_top, structure, lower, dinv):
    own = lower[0]
    half_id, low_id = lax.axis_index(HALF), lax.axis_index(LOW)
    row_id, col_id = lax.axis_index("row"), lax.axis_index("col")
    n_low, n_row, n_col = lax.axis_size(LOW), lax.axis_size("row"), lax.axis_size("col")
    groups = n_low * n_col
    per = TILE // groups
    n_ch = 2 if per % 16 == 0 else 1
    k = per // n_ch
    rt, width = sigma_top.shape[0] // TILE, sigma_top.shape[1]
    n_q = structure.shape[1]
    n_p = n_q // n_row
    s_rows, s_cols = own.shape

    near = half_id * n_low + (low_id ^ jnp.arange(n_low, dtype=jnp.int32))
    lists = jnp.take(structure, near, axis=0)
    mine = lax.dynamic_slice_in_dim(lists, row_id * n_p, n_p, axis=1)
    other = lax.dynamic_slice_in_dim(lists, (1 - row_id) * n_p, n_p, axis=1)
    cols = jnp.concatenate([mine, other], axis=1)

    parts = sigma_top.reshape(rt, groups, n_ch, k, width)
    got = []
    for ch in range(n_ch):
        send = parts[:, :, ch].transpose(1, 0, 2, 3)
        got.append(lax.all_to_all(send, (LOW, "col"), 0, 0, tiled=False))
    merge = max(1, TILE // width)
    if merge > 1:
        got = [
            g.reshape(groups // merge, merge, rt, k, width)
            .transpose(0, 2, 3, 1, 4)
            .reshape(groups // merge, rt, k, merge * width)
            for g in got
        ]

    own_x = swap(own, "col", 1)
    own_p = swap(own, "row", 1)

    s_mine, s_theirs = [], []
    panels = []
    for g in got:
        far = swap(g, HALF, 1)
        near_core = swap(g, "row", 1)
        far_core = swap(far, "row", 1)
        chosen = select((g, far, near_core, far_core), mine, cols, row_id, half_id, n_row)
        blocks = [chosen[0]] + [swap(chosen[s], LOW, s) for s in range(1, n_low)]
        panels.append(jnp.stack(blocks).reshape(-1, n_q * TILE))
    own_xp = swap(own_x, "row", 1)
    keep, sent = [], []
    for m in panels:
        a, b = m[:, :s_rows], m[:, s_rows:]
        out = -(dot(a, own_x) + dot(b, own_xp))
        sent.append(swap(out, "col", 1))
        keep.append(-(dot(a, own) + dot(b, own_p)))

    def place(blocks):
        full = [x.reshape(n_low, n_p, k, s_cols) for x in blocks]
        srcs = []
        for src in range(n_low):
            at = low_id ^ src
            srcs.append(
                jnp.stack(
                    [lax.dynamic_index_in_dim(x, at, 0, keepdims=False) for x in full], axis=1
                )
            )
        return jnp.stack(srcs, axis=1)

    kept, came = place(keep), place(sent)
    first = col_id == 0
    cross = jnp.stack([jnp.where(first, kept, came), jnp.where(first, came, kept)], axis=2)
    cross = cross.reshape(s_rows, s_cols)
    cross_p = swap(cross, "row", 1)
    same = row_id == col_id
    left = jnp.where(same, own, own_x)
    left_p = jnp.where(same, own_p, own_xp)
    dims = (((0,), (0,)), ((), ()))

    def tdot(a, b):
        return lax.dot_general(
            a, b, dims, precision=lax.Precision.HIGH, preferred_element_type=jnp.float32
        )

    front = dinv[0] - tdot(left, cross) - tdot(left_p, cross_p)
    return (cross[None], front[None])


def solution(mesh):
    n_leaf, n_row, n_col = (mesh.shape[a] for a in ("leaf", "row", "col"))
    fine = Mesh(
        mesh.devices.reshape(2, n_leaf // 2, n_row, n_col), (HALF, LOW, "row", "col")
    )
    leaf = (HALF, LOW)
    block = P(leaf, "row", "col")
    return jax.shard_map(
        body,
        mesh=fine,
        in_specs=(P("row", leaf + ("col",)), P(), block, block),
        out_specs=(block, block),
        check_vma=False,
    )
```

```python
import jax
import jax.numpy as jnp
from jax import lax
from jax.experimental import pallas as pl
from jax.experimental.pallas import tpu as pltpu
from jax.sharding import Mesh
from jax.sharding import PartitionSpec as P

TILE = 128
NEAR = 4
HALF = "half"
LOW = "low"
F32 = jnp.float32
BF16 = jnp.bfloat16


def swap(x, axis, bit):
    names = axis if isinstance(axis, tuple) else (axis,)
    size = 1
    for name in names:
        size *= lax.axis_size(name)
    return lax.ppermute(x, axis, [(i, i ^ bit) for i in range(size)])


def after(x, *deps):
    return lax.optimization_barrier((x,) + deps)[0]


def after_all(xs, *deps):
    return lax.optimization_barrier(tuple(xs) + deps)[: len(xs)]


def params(mib):
    return pltpu.CompilerParams(vmem_limit_bytes=mib << 20)


def cost(flops, *arrays):
    moved = sum(a.size * a.dtype.itemsize for a in arrays)
    return pl.CostEstimate(flops=flops, transcendentals=0, bytes_accessed=moved)


def any_spec():
    return pl.BlockSpec(memory_space=pl.ANY)


def like(shape, dtype=F32):
    return jax.ShapeDtypeStruct(shape, dtype)


def pack(parts):
    rt, groups, n_ch, k, width = parts.shape

    def kernel(src, out):
        for ch in range(n_ch):
            out[0, ch] = src[:, 0, ch]

    return pl.pallas_call(
        kernel,
        out_shape=like((groups, n_ch, rt, k, width)),
        grid=(groups,),
        in_specs=[pl.BlockSpec((rt, 1, n_ch, k, width), lambda i: (0, i, 0, 0, 0))],
        out_specs=pl.BlockSpec((1, n_ch, rt, k, width), lambda i: (i, 0, 0, 0, 0)),
        compiler_params=params(16),
        cost_estimate=cost(0, parts, parts),
    )(parts)


def select(pieces, chunk, rows, cols, row_id, half_id, n_half, cuts):
    n_src, rt, k, width = pieces[1].shape
    n_out, n_q = cols.shape
    n_p = rows.shape[1] // cuts
    per_src = width // TILE
    in_half = n_src * per_src
    n_pieces = len(pieces)
    src = cols % in_half // per_src
    row_at = ((rows // rt) ^ row_id) * (n_half * n_src * rt) + rows % rt
    col_at = ((cols // in_half) ^ half_id) * (n_src * rt) + src * rt
    lane_at = cols % per_src * TILE

    def kernel(row_at, col_at, lane_at, *refs):
        ins, outs = refs[:n_pieces], refs[n_pieces:-2]
        table, sems = refs[-2:]
        copies = []
        for i in range(n_pieces):
            piece = ins[i].at[:, chunk] if i % n_half == 0 else ins[i]
            copies.append(pltpu.make_async_copy(piece, table.at[i], sems.at[i]))
        for copy in copies:
            copy.start()
        for copy in copies:
            copy.wait()
        view = table.reshape(n_pieces * n_src * rt, k, width)
        for child in range(n_out):
            for q in range(n_q):
                base = col_at[child, q]
                lane = pl.multiple_of(lane_at[child, q], TILE)
                for p in range(n_p * cuts):
                    outs[p // n_p * n_out + child][p % n_p, :, q * TILE : (q + 1) * TILE] = view[
                        row_at[child, p] + base, :, pl.ds(lane, TILE)
                    ]

    out = like((n_p, k, n_q * TILE))
    flat = pl.pallas_call(
        kernel,
        out_shape=[out] * (n_out * cuts),
        grid_spec=pltpu.PrefetchScalarGridSpec(
            num_scalar_prefetch=3,
            grid=(1,),
            in_specs=[any_spec()] * n_pieces,
            out_specs=[pl.BlockSpec(out.shape, lambda i, *_: (0, 0, 0))] * (n_out * cuts),
            scratch_shapes=[
                pltpu.VMEM((n_pieces,) + pieces[1].shape, F32),
                pltpu.SemaphoreType.DMA((n_pieces,)),
            ],
        ),
        compiler_params=params(24),
        cost_estimate=cost(0, *pieces[1::2], *pieces[1::2], *[out] * (n_out * cuts)),
    )(row_at, col_at, lane_at, *pieces)
    return [flat[i * n_out : (i + 1) * n_out] for i in range(cuts)]


def halves(x):
    hi = x.astype(BF16)
    return hi, (x - hi.astype(F32)).astype(BF16)


def three(ah, al, bh, bl):
    d = lambda a, b: jnp.dot(a, b, preferred_element_type=F32)
    return d(ah, bh) + (d(ah, bl) + d(al, bh))


def split(top, bottom, block=256):
    rows, width = top.shape
    steps = rows // block

    def kernel(a, b, hi, lo):
        i = pl.program_id(0)

        @pl.when(i < steps)
        def _():
            hi[...], lo[...] = halves(a[...])

        @pl.when(i >= steps)
        def _():
            hi[...], lo[...] = halves(b[...])

    out = like((2 * rows, width), BF16)
    return pl.pallas_call(
        kernel,
        out_shape=[out, out],
        grid=(2 * steps,),
        in_specs=[
            pl.BlockSpec((block, width), lambda i: (jnp.minimum(i, steps - 1), 0)),
            pl.BlockSpec((block, width), lambda i: (jnp.maximum(i - steps, 0), 0)),
        ],
        out_specs=[pl.BlockSpec((block, width), lambda i: (i, 0))] * 2,
        compiler_params=params(16),
        cost_estimate=cost(0, top, bottom, out, out),
    )(top, bottom)


def turn(blocks, shape, col_id, same):
    n_p, n_low, n_col, n_ch, k = shape
    width = blocks[0].shape[1]
    deep = n_p * n_low * k
    views = [b.reshape(n_p, n_low, n_col, n_ch, k, width) for b in blocks]
    flags = jnp.stack([col_id, same.astype(jnp.int32)])
    half_p = n_p // 2
    pieces = [[(core, far, 0, 0, n_p)] for core in range(2) for far in range(n_col)]
    pieces += [
        [(core, far, 1, unit * half_p, half_p) for core in range(2)]
        for far in range(n_col)
        for unit in range(2)
    ]
    moves = []
    for at, piece in enumerate(pieces):
        row = 0
        for core, far, ch, tile, tiles in piece:
            moves.append((at, row, core, far, ch, tile, tiles))
            row += tiles

    def kernel(flag, own, own_p, far, far_p, hi, lo, buf, sems):
        i = pl.program_id(0)

        @pl.when(i == 0)
        def _():
            for use, refs in ((1, (own, own_p)), (0, (far, far_p))):

                @pl.when(flag[1] == use)
                def _(refs=refs):
                    for at, row, core, side, ch, tile, tiles in moves:
                        pltpu.make_async_copy(
                            refs[core].at[pl.ds(tile, tiles), :, flag[0] ^ side, ch],
                            buf.at[at, pl.ds(row, tiles)],
                            sems.at[at],
                        ).start()

        pltpu.make_async_copy(own.at[:, :, flag[0], 0], buf.at[i], sems.at[i]).wait()
        hi[0], lo[0] = halves(buf[i].reshape(deep, width).T)

    out = like((len(pieces), width, deep), BF16)
    return pl.pallas_call(
        kernel,
        out_shape=[out, out],
        grid_spec=pltpu.PrefetchScalarGridSpec(
            num_scalar_prefetch=1,
            grid=(len(pieces),),
            in_specs=[any_spec()] * 4,
            out_specs=[pl.BlockSpec((1, width, deep), lambda i, *_: (i, 0, 0))] * 2,
            scratch_shapes=[
                pltpu.VMEM((len(pieces), n_p, n_low, k, width), F32),
                pltpu.SemaphoreType.DMA((len(pieces),)),
            ],
        ),
        compiler_params=params(32),
        cost_estimate=cost(0, blocks[0], blocks[0], out, out),
    )(flags, *views)


def panel(blocks, low_id):
    n_low = len(blocks)
    n_p, k, deep = blocks[0].shape
    rows = n_p * n_low * k

    def kernel(at, *refs):
        ins, (mh, ml, full) = refs[:n_low], refs[n_low:]
        for s in range(n_low):
            full[:, at[0] ^ s] = ins[s][...]
        mh[...], ml[...] = halves(full[...].reshape(rows, -1))

    out = like((rows, deep), BF16)
    wide = deep // 4
    return pl.pallas_call(
        kernel,
        out_shape=[out, out],
        grid_spec=pltpu.PrefetchScalarGridSpec(
            num_scalar_prefetch=1,
            grid=(deep // wide,),
            in_specs=[pl.BlockSpec((n_p, k, wide), lambda i, *_: (0, 0, i))] * n_low,
            out_specs=[pl.BlockSpec((rows, wide), lambda i, *_: (0, i))] * 2,
            scratch_shapes=[pltpu.VMEM((n_p, n_low, k, wide), F32)],
        ),
        compiler_params=params(16),
        cost_estimate=cost(0, *blocks, *blocks),
    )(low_id.reshape(1), *blocks)


def product(mh, ml, parts, shape, wide=256):
    rows, deep = mh.shape
    _, n_low, _, _, k = shape
    n_p = rows // (n_low * k)
    steps = parts[0][0].shape[1] // wide
    n = len(parts)

    def kernel(mh, ml, *refs):
        out = refs[-1]
        for j in range(n):

            @pl.when(pl.program_id(0) // steps == j)
            def _(j=j):
                hi, lo = refs[2 * j : 2 * j + 2]
                new = -three(mh[...], ml[...], hi[...], lo[...])
                out[...] = new.reshape(n_p, n_low, k, wide)

    out = like((n_p, n_low, k, n * steps * wide))
    whole = pl.BlockSpec((rows, deep), lambda i: (0, 0))
    specs, args = [whole, whole], [mh, ml]
    for j, part in enumerate(parts):
        strip = pl.BlockSpec(
            (deep, wide), lambda i, j=j: (0, jnp.clip(i - j * steps, 0, steps - 1))
        )
        specs += [strip, strip]
        args += part
    return pl.pallas_call(
        kernel,
        out_shape=out,
        grid=(n * steps,),
        in_specs=specs,
        out_specs=pl.BlockSpec((n_p, n_low, k, wide), lambda i: (0, 0, 0, i)),
        compiler_params=params(32),
        cost_estimate=cost(6 * rows * deep * n * steps * wide, *args, out),
    )(*args)


def update(base, turned, pieces, in_place, wide=256):
    height, width = base.shape
    n = len(pieces)
    tall = height // 2
    strip = pl.BlockSpec((height, wide), lambda i: (0, i))
    specs, args, plan = [strip], [base], []
    for at, blocks in pieces:
        for part in turned:
            for x in part:
                deep = x.shape[2]
                specs.append(pl.BlockSpec((1, tall, deep), lambda i, at=at: (at, 0, 0)))
                args.append(x)
        for columns in blocks:
            steps = columns[0].shape[-1] // wide
            plan.append((len(blocks), len(columns), steps))
            for j, x in enumerate(columns):
                x = x.reshape(-1, x.shape[-1])
                specs.append(
                    pl.BlockSpec(
                        (x.shape[0], wide),
                        lambda i, j=j, steps=steps: (0, jnp.clip(i - j * steps, 0, steps - 1)),
                    )
                )
                args.append(x)
    n_in = len(args)

    def kernel(*refs):
        acc, out = refs[0], refs[n_in]
        where = pl.program_id(0)
        top, bottom = acc[:tall], acc[tall:]
        at, row = 1, 0
        for _ in range(n):
            upper, lower_ = refs[at : at + 2], refs[at + 2 : at + 4]
            at += 4
            rows = []
            for _ in range(plan[row][0]):
                _, columns, steps = plan[row]
                x = refs[at][...]
                for j in range(1, columns):
                    x = jnp.where(where // steps == j, refs[at + j][...], x)
                rows.append(x)
                at += columns
                row += 1
            sh, sl = halves(rows[0] if len(rows) == 1 else jnp.concatenate(rows, axis=0))
            top = top - three(upper[0][0], upper[1][0], sh, sl)
            bottom = bottom - three(lower_[0][0], lower_[1][0], sh, sl)
        out[:tall], out[tall:] = top, bottom

    deep = turned[0][0].shape[2] * n
    return pl.pallas_call(
        kernel,
        out_shape=like(base.shape),
        grid=(width // wide,),
        in_specs=specs,
        out_specs=strip,
        input_output_aliases={0: 0} if in_place else {},
        compiler_params=params(40),
        cost_estimate=cost(6 * height * deep * width, base, base),
    )(*args)


def place(pieces, into, shape, col_id, width):
    n_p, n_low, n_col, n_ch, k = shape
    n = len(pieces)

    def kernel(at, *refs):
        ins, out, sems = refs[:n], refs[-2], refs[-1]
        copies = []
        for i, (rows, tile, far, ch, start) in enumerate(pieces):
            tiles, cols = pl.ds(tile, rows.shape[0]), pl.ds(start, rows.shape[-1])
            spot = out.at[tiles, :, at[0] ^ far, ch, :, cols]
            copies.append(pltpu.make_async_copy(ins[i], spot, sems.at[i]))
        for copy in copies:
            copy.start()
        for copy in copies:
            copy.wait()

    args = [x[0] for x in pieces]
    specs = [pl.BlockSpec(memory_space=pltpu.VMEM)] * n
    aliases = {}
    if into is not None:
        args.append(into)
        specs.append(any_spec())
        aliases = {n + 1: 0}
    return pl.pallas_call(
        kernel,
        out_shape=like((n_p, n_low, n_col, n_ch, k, width)),
        grid_spec=pltpu.PrefetchScalarGridSpec(
            num_scalar_prefetch=1,
            in_specs=specs,
            out_specs=any_spec(),
            scratch_shapes=[pltpu.SemaphoreType.DMA((n,))],
        ),
        input_output_aliases=aliases,
        compiler_params=params(16),
        cost_estimate=cost(0, *args[:n], *args[:n]),
    )(col_id.reshape(1), *args)


def body(sigma_top, structure, lower, dinv):
    own = lower[0]
    half_id, low_id = lax.axis_index(HALF), lax.axis_index(LOW)
    row_id, col_id = lax.axis_index("row"), lax.axis_index("col")
    n_half, n_low = lax.axis_size(HALF), lax.axis_size(LOW)
    n_row, n_col = lax.axis_size("row"), lax.axis_size("col")
    groups = n_low * n_col
    n_ch = 2
    k = TILE // groups // n_ch
    rt, width = sigma_top.shape[0] // TILE, sigma_top.shape[1]
    n_q = structure.shape[1]
    n_p = n_q // n_row
    near_id = low_id * n_col + col_id

    children = half_id * n_low + (low_id ^ jnp.arange(n_low, dtype=jnp.int32))
    lists = jnp.take(structure, children, axis=0)
    mine = lax.dynamic_slice_in_dim(lists, row_id * n_p, n_p, axis=1)
    other = lax.dynamic_slice_in_dim(lists, (1 - row_id) * n_p, n_p, axis=1)
    cols = jnp.concatenate([mine, other], axis=1)

    parts = sigma_top.reshape(rt, groups, n_ch, k, width)
    got = lax.all_to_all(pack(parts), (LOW, "col"), 0, 0)
    cut = own.shape[1] // 2
    far = [swap(after(own[:, i * cut : (i + 1) * cut], got), "col", 1) for i in range(2)]
    own_p = swap(own, "row", 1)
    merge = max(1, TILE // width)
    if merge > 1:
        got = (
            got.reshape(groups // merge, merge, n_ch, rt, k, width)
            .transpose(0, 2, 3, 4, 1, 5)
            .reshape(groups // merge, n_ch, rt, k, merge * width)
        )
    got_p = swap(got, "row", 1)
    shape = (n_p, n_low, n_col, n_ch, k)

    def others(chunk):
        return [swap(chunk, HALF, s) for s in range(1, n_half)]

    def choose(got, ring, ch, cuts):
        pieces = [got] + ring + [got_p] + [swap(x, "row", 1) for x in ring]
        return select(pieces, ch, mine, cols, row_id, half_id, n_half, cuts)

    def hand_out(chosen):
        return [chosen[0]] + [swap(chosen[s], LOW, s) for s in range(1, n_low)]

    same = row_id == col_id
    near = split(own, own_p)
    ring = others(got[:, 0])
    ring[-1] = after(ring[-1], near[0])
    far[0] = after(far[0], ring[-1])
    far_p = [swap(far[0], "row", 1)]
    (chosen,) = choose(got, ring, 0, 1)
    blocks = hand_out(chosen)
    far_parts = [split(after(far[0], chosen[0]), far_p[0])]
    turned = [turn((own[:, :cut], own_p[:, :cut], far[0], far_p[0]), shape, col_id, same)]
    ring = others(after(got[:, 1], chosen[0]))
    ring[-1] = after(ring[-1], far_parts[0][0], turned[0][0])
    far[1], *blocks = after_all((far[1], *blocks), ring[-1])
    far_p.append(swap(far[1], "row", 1))
    first = panel(blocks, low_id)
    sent = product(*first, far_parts[:1], shape)
    came = [(swap(sent, "col", 1), 0, 0, 0)]
    chosen = choose(after(got, sent), ring, 1, 2)
    units = [hand_out(x) for x in chosen]
    far_parts.append(split(after(far[1], chosen[0][0]), far_p[1]))
    sent = product(*first, far_parts[1:], shape)
    came.append((swap(sent, "col", 1), 0, 0, cut))
    kept = [(product(after(first[0], sent), first[1], [near], shape), 0, 0, 0)]
    for i, unit in enumerate(units):
        m = panel([after(x, kept[0][0]) for x in unit], low_id)
        sent = product(*m, far_parts, shape)
        tile = i * n_p // 2
        came.append((swap(sent, "col", 1), tile, 1, 0))
        kept.append((product(after(m[0], sent), m[1], [near], shape), tile, 1, 0))
        if i == 0:
            turned.append(
                turn(
                    (after(own, kept[-1][0])[:, cut:], own_p[:, cut:], far[1], far_p[1]),
                    shape,
                    col_id,
                    same,
                )
            )

    def pair(x):
        return [x[0]], [swap(x[0], "row", 1)]

    mine_a, peer_a = pair(kept[0])
    came_a = [came[0][0], came[1][0]]
    came_ap = [swap(x, "row", 1) for x in came_a]
    base = n_row * n_col
    front = update(
        dinv[0],
        turned,
        [(0, [mine_a]), (1, [came_a]), (n_col, [peer_a]), (n_col + 1, [came_ap])],
        False,
    )
    front = update(
        front,
        turned,
        [(base, pair(kept[1])), (base + 1, pair(kept[2])), (base + 2, pair(came[2]))],
        True,
    )
    front = update(front, turned, [(base + 3, pair(came[3]))], True)
    cross = None
    for group in (
        [(r, t, 0, c, x) for r, t, c, x in kept] + [(r, t, 1, c, x) for r, t, c, x in came[:3]],
        [(r, t, 1, c, x) for r, t, c, x in came[3:]],
    ):
        cross = place(group, cross, shape, col_id, own.shape[1])
    return (cross.reshape(own.shape)[None], front[None])


def solution(mesh):
    n_leaf, n_row, n_col = (mesh.shape[a] for a in ("leaf", "row", "col"))
    fine = Mesh(
        mesh.devices.reshape(n_leaf // NEAR, NEAR, n_row, n_col), (HALF, LOW, "row", "col")
    )
    leaf = (HALF, LOW)
    block = P(leaf, "row", "col")
    return jax.shard_map(
        body,
        mesh=fine,
        in_specs=(P("row", leaf + ("col",)), P(), block, block),
        out_specs=(block, block),
        check_vma=False,
    )
```

```python
import jax
import jax.numpy as jnp
from jax import lax
from jax.experimental import pallas as pl
from jax.experimental.pallas import tpu as pltpu
from jax.sharding import Mesh
from jax.sharding import PartitionSpec as P

TILE = 128
NEAR = 4
HALF = "half"
LOW = "low"
F32 = jnp.float32
BF16 = jnp.bfloat16


def swap(x, axis, bit):
    names = axis if isinstance(axis, tuple) else (axis,)
    size = 1
    for name in names:
        size *= lax.axis_size(name)
    return lax.ppermute(x, axis, [(i, i ^ bit) for i in range(size)])


def after(x, *deps):
    return lax.optimization_barrier((x,) + deps)[0]


def after_all(xs, *deps):
    return lax.optimization_barrier(tuple(xs) + deps)[: len(xs)]


def params(mib):
    return pltpu.CompilerParams(vmem_limit_bytes=mib << 20)


def cost():
    return pl.CostEstimate(flops=1, transcendentals=0, bytes_accessed=1)


def any_spec():
    return pl.BlockSpec(memory_space=pl.ANY)


def like(shape, dtype=F32):
    return jax.ShapeDtypeStruct(shape, dtype)


def pack(parts):
    rt, groups, n_ch, k, width = parts.shape

    def kernel(src, out):
        for ch in range(n_ch):
            out[0, ch] = src[:, 0, ch]

    return pl.pallas_call(
        kernel,
        out_shape=like((groups, n_ch, rt, k, width)),
        grid=(groups,),
        in_specs=[pl.BlockSpec((rt, 1, n_ch, k, width), lambda i: (0, i, 0, 0, 0))],
        out_specs=pl.BlockSpec((1, n_ch, rt, k, width), lambda i: (i, 0, 0, 0, 0)),
        compiler_params=params(16),
        cost_estimate=cost(),
    )(parts)


def select(pieces, chunk, rows, cols, row_id, half_id, n_half, cuts):
    n_src, rt, k, width = pieces[1].shape
    n_out, n_q = cols.shape
    n_p = rows.shape[1] // cuts
    per_src = width // TILE
    in_half = n_src * per_src
    n_pieces = len(pieces)
    src = cols % in_half // per_src
    row_at = ((rows // rt) ^ row_id) * (n_half * n_src * rt) + rows % rt
    col_at = ((cols // in_half) ^ half_id) * (n_src * rt) + src * rt
    lane_at = cols % per_src * TILE

    def kernel(row_at, col_at, lane_at, *refs):
        ins, outs = refs[:n_pieces], refs[n_pieces:-2]
        table, sems = refs[-2:]
        copies = []
        for i in range(n_pieces):
            piece = ins[i].at[:, chunk] if i % n_half == 0 else ins[i]
            copies.append(pltpu.make_async_copy(piece, table.at[i], sems.at[i]))
        for copy in copies:
            copy.start()
        for copy in copies:
            copy.wait()
        view = table.reshape(n_pieces * n_src * rt, k, width)
        for child in range(n_out):
            for q in range(n_q):
                base = col_at[child, q]
                lane = pl.multiple_of(lane_at[child, q], TILE)
                for p in range(n_p * cuts):
                    outs[p // n_p * n_out + child][p % n_p, :, q * TILE : (q + 1) * TILE] = view[
                        row_at[child, p] + base, :, pl.ds(lane, TILE)
                    ]

    out = like((n_p, k, n_q * TILE))
    flat = pl.pallas_call(
        kernel,
        out_shape=[out] * (n_out * cuts),
        grid_spec=pltpu.PrefetchScalarGridSpec(
            num_scalar_prefetch=3,
            grid=(1,),
            in_specs=[any_spec()] * n_pieces,
            out_specs=[pl.BlockSpec(out.shape, lambda i, *_: (0, 0, 0))] * (n_out * cuts),
            scratch_shapes=[
                pltpu.VMEM((n_pieces,) + pieces[1].shape, F32),
                pltpu.SemaphoreType.DMA((n_pieces,)),
            ],
        ),
        compiler_params=params(24),
        cost_estimate=cost(),
    )(row_at, col_at, lane_at, *pieces)
    return [flat[i * n_out : (i + 1) * n_out] for i in range(cuts)]


def halves(x):
    hi = x.astype(BF16)
    return hi, (x - hi.astype(F32)).astype(BF16)


def three(ah, al, bh, bl):
    d = lambda a, b: jnp.dot(a, b, preferred_element_type=F32)
    return d(ah, bh) + (d(ah, bl) + d(al, bh))


def split(top, bottom, block=256):
    rows, width = top.shape
    steps = rows // block

    def kernel(a, b, hi, lo):
        i = pl.program_id(0)

        @pl.when(i < steps)
        def _():
            hi[...], lo[...] = halves(a[...])

        @pl.when(i >= steps)
        def _():
            hi[...], lo[...] = halves(b[...])

    out = like((2 * rows, width), BF16)
    return pl.pallas_call(
        kernel,
        out_shape=[out, out],
        grid=(2 * steps,),
        in_specs=[
            pl.BlockSpec((block, width), lambda i: (jnp.minimum(i, steps - 1), 0)),
            pl.BlockSpec((block, width), lambda i: (jnp.maximum(i - steps, 0), 0)),
        ],
        out_specs=[pl.BlockSpec((block, width), lambda i: (i, 0))] * 2,
        compiler_params=params(16),
        cost_estimate=cost(),
    )(top, bottom)


def turn(blocks, shape, col_id, same):
    n_p, n_low, n_col, n_ch, k = shape
    width = blocks[0].shape[1]
    deep = n_p * n_low * k
    views = [b.reshape(n_p, n_low, n_col, n_ch, k, width) for b in blocks]
    flags = jnp.stack([col_id, same.astype(jnp.int32)])
    half_p = n_p // 2
    pieces = [[(core, far, 0, 0, n_p)] for core in range(2) for far in range(n_col)]
    pieces += [[(core, 0, 1, 0, n_p)] for core in range(2)]
    pieces += [[(core, 1, 1, 0, n_p)] for core in range(2)]
    moves = []
    for at, piece in enumerate(pieces):
        row = 0
        for core, far, ch, tile, tiles in piece:
            moves.append((at, row, core, far, ch, tile, tiles))
            row += tiles

    def kernel(flag, own, own_p, far, far_p, hi, lo, buf, sems):
        i = pl.program_id(0)

        @pl.when(i == 0)
        def _():
            for use, refs in ((1, (own, own_p)), (0, (far, far_p))):

                @pl.when(flag[1] == use)
                def _(refs=refs):
                    for at, row, core, side, ch, tile, tiles in moves:
                        pltpu.make_async_copy(
                            refs[core].at[pl.ds(tile, tiles), :, flag[0] ^ side, ch],
                            buf.at[at, pl.ds(row, tiles)],
                            sems.at[at],
                        ).start()

        pltpu.make_async_copy(own.at[:, :, flag[0], 0], buf.at[i], sems.at[i]).wait()
        hi[0], lo[0] = halves(buf[i].reshape(deep, width).T)

    out = like((len(pieces), width, deep), BF16)
    return pl.pallas_call(
        kernel,
        out_shape=[out, out],
        grid_spec=pltpu.PrefetchScalarGridSpec(
            num_scalar_prefetch=1,
            grid=(len(pieces),),
            in_specs=[any_spec()] * 4,
            out_specs=[pl.BlockSpec((1, width, deep), lambda i, *_: (i, 0, 0))] * 2,
            scratch_shapes=[
                pltpu.VMEM((len(pieces), n_p, n_low, k, width), F32),
                pltpu.SemaphoreType.DMA((len(pieces),)),
            ],
        ),
        compiler_params=params(32),
        cost_estimate=cost(),
    )(flags, *views)


def panel(blocks, low_id):
    n_low = len(blocks)
    n_p, k, deep = blocks[0].shape
    rows = n_p * n_low * k

    def kernel(at, *refs):
        ins, (mh, ml, full) = refs[:n_low], refs[n_low:]
        for s in range(n_low):
            full[:, at[0] ^ s] = ins[s][...]
        mh[...], ml[...] = halves(full[...].reshape(rows, -1))

    out = like((rows, deep), BF16)
    wide = deep // 4
    return pl.pallas_call(
        kernel,
        out_shape=[out, out],
        grid_spec=pltpu.PrefetchScalarGridSpec(
            num_scalar_prefetch=1,
            grid=(deep // wide,),
            in_specs=[pl.BlockSpec((n_p, k, wide), lambda i, *_: (0, 0, i))] * n_low,
            out_specs=[pl.BlockSpec((rows, wide), lambda i, *_: (0, i))] * 2,
            scratch_shapes=[pltpu.VMEM((n_p, n_low, k, wide), F32)],
        ),
        compiler_params=params(16),
        cost_estimate=cost(),
    )(low_id.reshape(1), *blocks)


def product(panels, parts, shape, wide=256):
    deep = panels[0][0].shape[1]
    _, n_low, _, _, k = shape
    tiles = [m[0].shape[0] // (n_low * k) for m in panels]
    n_p = sum(tiles)
    rows = n_p * n_low * k
    steps = parts[0][0].shape[1] // wide
    n, n_m = len(parts), len(panels)

    def kernel(*refs):
        out = refs[-1]
        for j in range(n):

            @pl.when(pl.program_id(0) // steps == j)
            def _(j=j):
                hi, lo = refs[2 * n_m + 2 * j : 2 * n_m + 2 * j + 2]
                tile = 0
                for i in range(n_m):
                    mh, ml = refs[2 * i : 2 * i + 2]
                    new = -three(mh[...], ml[...], hi[...], lo[...])
                    out[tile : tile + tiles[i]] = new.reshape(tiles[i], n_low, k, wide)
                    tile += tiles[i]

    out = like((n_p, n_low, k, n * steps * wide))
    specs, args = [], []
    for m in panels:
        specs += [pl.BlockSpec(m[0].shape, lambda i: (0, 0))] * 2
        args += m
    for j, part in enumerate(parts):
        strip = pl.BlockSpec(
            (deep, wide), lambda i, j=j: (0, jnp.clip(i - j * steps, 0, steps - 1))
        )
        specs += [strip, strip]
        args += part
    return pl.pallas_call(
        kernel,
        out_shape=out,
        grid=(n * steps,),
        in_specs=specs,
        out_specs=pl.BlockSpec((n_p, n_low, k, wide), lambda i: (0, 0, 0, i)),
        compiler_params=params(32),
        cost_estimate=cost(),
    )(*args)


def update(base, turned, pieces, in_place, wide=256):
    height, width = base.shape
    n = len(pieces)
    tall = height // 2
    strip = pl.BlockSpec((height, wide), lambda i: (0, i))
    specs, args, plan = [strip], [base], []
    for at, blocks in pieces:
        for part in turned:
            for x in part:
                deep = x.shape[2]
                specs.append(pl.BlockSpec((1, tall, deep), lambda i, at=at: (at, 0, 0)))
                args.append(x)
        for columns in blocks:
            columns = [x if isinstance(x, tuple) else (x, None) for x in columns]
            steps = columns[0][0].shape[-1] // wide
            plan.append((len(blocks), len(columns), steps))
            for j, (x, row) in enumerate(columns):
                x = x.reshape(-1, x.shape[-1])
                specs.append(
                    pl.BlockSpec(
                        (x.shape[0] if row is None else turned[0][0].shape[2], wide),
                        lambda i, j=j, steps=steps, row=row or 0: (
                            row,
                            jnp.clip(i - j * steps, 0, steps - 1),
                        ),
                    )
                )
                args.append(x)
    n_in = len(args)

    def kernel(*refs):
        acc, out = refs[0], refs[n_in]
        where = pl.program_id(0)
        top, bottom = acc[:tall], acc[tall:]
        at, row = 1, 0
        for _ in range(n):
            upper, lower_ = refs[at : at + 2], refs[at + 2 : at + 4]
            at += 4
            rows = []
            for _ in range(plan[row][0]):
                _, columns, steps = plan[row]
                x = refs[at][...]
                for j in range(1, columns):
                    x = jnp.where(where // steps == j, refs[at + j][...], x)
                rows.append(x)
                at += columns
                row += 1
            sh, sl = halves(rows[0] if len(rows) == 1 else jnp.concatenate(rows, axis=0))
            top = top - three(upper[0][0], upper[1][0], sh, sl)
            bottom = bottom - three(lower_[0][0], lower_[1][0], sh, sl)
        out[:tall], out[tall:] = top, bottom

    deep = turned[0][0].shape[2] * n
    return pl.pallas_call(
        kernel,
        out_shape=like(base.shape),
        grid=(width // wide,),
        in_specs=specs,
        out_specs=strip,
        input_output_aliases={0: 0} if in_place else {},
        compiler_params=params(40),
        cost_estimate=cost(),
    )(*args)


def place(pieces, into, shape, col_id, width):
    n_p, n_low, n_col, n_ch, k = shape
    n = len(pieces)

    def kernel(at, *refs):
        ins, out, sems = refs[:n], refs[-2], refs[-1]
        copies = []
        for i, (rows, skip, count, tile, far, ch, start) in enumerate(pieces):
            tiles, cols = pl.ds(tile, count), pl.ds(start, rows.shape[-1])
            spot = out.at[tiles, :, at[0] ^ far, ch, :, cols]
            copies.append(
                pltpu.make_async_copy(ins[i].at[pl.ds(skip, count)], spot, sems.at[i])
            )
        for copy in copies:
            copy.start()
        for copy in copies:
            copy.wait()

    args = [x[0] for x in pieces]
    specs = [pl.BlockSpec(memory_space=pltpu.VMEM)] * n
    aliases = {}
    if into is not None:
        args.append(into)
        specs.append(any_spec())
        aliases = {n + 1: 0}
    return pl.pallas_call(
        kernel,
        out_shape=like((n_p, n_low, n_col, n_ch, k, width)),
        grid_spec=pltpu.PrefetchScalarGridSpec(
            num_scalar_prefetch=1,
            in_specs=specs,
            out_specs=any_spec(),
            scratch_shapes=[pltpu.SemaphoreType.DMA((n,))],
        ),
        input_output_aliases=aliases,
        compiler_params=params(16),
        cost_estimate=cost(),
    )(col_id.reshape(1), *args)


def body(sigma_top, structure, lower, dinv):
    own = lower[0]
    half_id, low_id = lax.axis_index(HALF), lax.axis_index(LOW)
    row_id, col_id = lax.axis_index("row"), lax.axis_index("col")
    n_half, n_low = lax.axis_size(HALF), lax.axis_size(LOW)
    n_row, n_col = lax.axis_size("row"), lax.axis_size("col")
    groups = n_low * n_col
    n_ch = 2
    k = TILE // groups // n_ch
    rt, width = sigma_top.shape[0] // TILE, sigma_top.shape[1]
    n_q = structure.shape[1]
    n_p = n_q // n_row
    near_id = low_id * n_col + col_id

    children = half_id * n_low + (low_id ^ jnp.arange(n_low, dtype=jnp.int32))
    lists = jnp.take(structure, children, axis=0)
    mine = lax.dynamic_slice_in_dim(lists, row_id * n_p, n_p, axis=1)
    other = lax.dynamic_slice_in_dim(lists, (1 - row_id) * n_p, n_p, axis=1)
    cols = jnp.concatenate([mine, other], axis=1)

    parts = sigma_top.reshape(rt, groups, n_ch, k, width)
    got = lax.all_to_all(pack(parts), (LOW, "col"), 0, 0)
    cut = own.shape[1] // 2
    far = [swap(after(own[:, i * cut : (i + 1) * cut], got), "col", 1) for i in range(2)]
    own_p = swap(own, "row", 1)
    merge = max(1, TILE // width)
    if merge > 1:
        got = (
            got.reshape(groups // merge, merge, n_ch, rt, k, width)
            .transpose(0, 2, 3, 4, 1, 5)
            .reshape(groups // merge, n_ch, rt, k, merge * width)
        )
    got_p = swap(got, "row", 1)
    shape = (n_p, n_low, n_col, n_ch, k)

    def others(chunk):
        return [swap(chunk, HALF, s) for s in range(1, n_half)]

    def choose(got, ring, ch, cuts):
        pieces = [got] + ring + [got_p] + [swap(x, "row", 1) for x in ring]
        return select(pieces, ch, mine, cols, row_id, half_id, n_half, cuts)

    def hand_out(chosen):
        return [chosen[0]] + [swap(chosen[s], LOW, s) for s in range(1, n_low)]

    same = row_id == col_id
    own_c = [own[:, i * cut : (i + 1) * cut] for i in range(2)]
    own_pc = [own_p[:, i * cut : (i + 1) * cut] for i in range(2)]
    near = [split(x, y) for x, y in zip(own_c, own_pc)]
    ring = others(got[:, 0])
    ring[-1] = after(ring[-1], near[0][0], near[1][0])
    far[0] = after(far[0], ring[-1])
    far_p = [swap(far[0], "row", 1)]
    (chosen,) = choose(got, ring, 0, 1)
    blocks = hand_out(chosen)
    far_parts = [split(after(far[0], chosen[0]), far_p[0])]
    turned = [turn((own_c[0], own_pc[0], far[0], far_p[0]), shape, col_id, same)]
    ring = others(after(got[:, 1], ring[-1]))
    ring[-1] = after(ring[-1], far_parts[0][0], turned[0][0])
    far[1], *blocks = after_all((far[1], *blocks), ring[-1])
    far_p.append(swap(far[1], "row", 1))
    first = panel(blocks, low_id)
    sent = product([first], far_parts[:1], shape)
    came = [(swap(sent, "col", 1), 0, 0, 0)]
    chosen = choose(after(got, sent), ring, 1, 1)
    units = [hand_out(x) for x in chosen]
    far_parts.append(split(after(far[1], chosen[0][0]), far_p[1]))
    last = product([first], far_parts[1:], shape)
    came.append((swap(last, "col", 1), 0, 0, cut))
    turned.append(
        turn((after(own_c[1], last), own_pc[1], far[1], far_p[1]), shape, col_id, same)
    )
    kept = [[product([after_all(first, turned[1][0])], near, shape)]]
    second = panel(after_all(units[0], kept[0][0], came[1][0]), low_id)
    last = product([second], far_parts, shape)
    came.append((swap(last, "col", 1), 0, 1, 0))
    came_p = [swap(after(came[i][0], last), "row", 1) for i in range(2)]
    second = after_all(second, last)
    kept.append([product([second], [x], shape) for x in near])
    kept_p = [[swap(after(x, last), "row", 1) for x in xs] for xs in kept]

    def other_core(x):
        return swap(x, "row", 1)

    base = n_row * n_col
    front = update(
        dinv[0],
        turned,
        [
            (0, [kept[0]]),
            (n_col, [kept_p[0]]),
            (base, [kept[1]]),
            (base + 1, [kept_p[1]]),
            (1, [[came[0][0], came[1][0]]]),
            (n_col + 1, [came_p]),
        ],
        False,
    )
    end = after(came[2][0], front)
    front = update(
        front, turned, [(base + 2, [[end]]), (base + 3, [[other_core(end)]])], True
    )
    cross = None
    for group in (
        [(kept[ch][i], 0, n_p, 0, 0, ch, i * cut) for ch in range(n_ch) for i in range(len(kept[ch]))]
        + [(r, 0, r.shape[0], t, 1, c, x) for r, t, c, x in came[:2]],
        [(r, 0, r.shape[0], t, 1, c, x) for r, t, c, x in came[2:]],
    ):
        cross = place(group, cross, shape, col_id, own.shape[1])
    return (cross.reshape(own.shape)[None], front[None])


def solution(mesh):
    n_leaf, n_row, n_col = (mesh.shape[a] for a in ("leaf", "row", "col"))
    fine = Mesh(
        mesh.devices.reshape(n_leaf // NEAR, NEAR, n_row, n_col), (HALF, LOW, "row", "col")
    )
    leaf = (HALF, LOW)
    block = P(leaf, "row", "col")
    return jax.shard_map(
        body,
        mesh=fine,
        in_specs=(P("row", leaf + ("col",)), P(), block, block),
        out_specs=(block, block),
        check_vma=False,
    )
```

```python
import jax
import jax.numpy as jnp
from jax import lax
from jax.experimental import pallas as pl
from jax.experimental.pallas import tpu as pltpu
from jax.sharding import Mesh
from jax.sharding import PartitionSpec as P

TILE = 128
NEAR = 4
HALF = "half"
LOW = "low"
F32 = jnp.float32
BF16 = jnp.bfloat16


def swap(x, axis, bit):
    names = axis if isinstance(axis, tuple) else (axis,)
    size = 1
    for name in names:
        size *= lax.axis_size(name)
    return lax.ppermute(x, axis, [(i, i ^ bit) for i in range(size)])


def after(x, *deps):
    return lax.optimization_barrier((x,) + deps)[0]


def after_all(xs, *deps):
    return lax.optimization_barrier(tuple(xs) + deps)[: len(xs)]


def params(mib):
    return pltpu.CompilerParams(vmem_limit_bytes=mib << 20)


def cost():
    return pl.CostEstimate(flops=1, transcendentals=0, bytes_accessed=1)


def any_spec():
    return pl.BlockSpec(memory_space=pl.ANY)


def like(shape, dtype=F32):
    return jax.ShapeDtypeStruct(shape, dtype)


def pack(parts):
    rt, groups, n_ch, k, width = parts.shape

    def kernel(src, out):
        for ch in range(n_ch):
            out[0, ch] = src[:, 0, ch]

    return pl.pallas_call(
        kernel,
        out_shape=like((groups, n_ch, rt, k, width)),
        grid=(groups,),
        in_specs=[pl.BlockSpec((rt, 1, n_ch, k, width), lambda i: (0, i, 0, 0, 0))],
        out_specs=pl.BlockSpec((1, n_ch, rt, k, width), lambda i: (i, 0, 0, 0, 0)),
        compiler_params=params(16),
        cost_estimate=cost(),
    )(parts)


def select(pieces, chunk, rows, cols, row_id, half_id, n_half, cuts):
    n_src, rt, k, width = pieces[1].shape
    n_out, n_q = cols.shape
    n_p = rows.shape[1] // cuts
    per_src = width // TILE
    in_half = n_src * per_src
    n_pieces = len(pieces)
    src = cols % in_half // per_src
    row_at = ((rows // rt) ^ row_id) * (n_half * n_src * rt) + rows % rt
    col_at = ((cols // in_half) ^ half_id) * (n_src * rt) + src * rt
    lane_at = cols % per_src * TILE

    def kernel(row_at, col_at, lane_at, *refs):
        ins, outs = refs[:n_pieces], refs[n_pieces:-2]
        table, sems = refs[-2:]
        copies = []
        for i in range(n_pieces):
            piece = ins[i].at[:, chunk] if i % n_half == 0 else ins[i]
            copies.append(pltpu.make_async_copy(piece, table.at[i], sems.at[i]))
        for copy in copies:
            copy.start()
        for copy in copies:
            copy.wait()
        view = table.reshape(n_pieces * n_src * rt, k, width)
        for child in range(n_out):
            for q in range(n_q):
                base = col_at[child, q]
                lane = pl.multiple_of(lane_at[child, q], TILE)
                for p in range(n_p * cuts):
                    outs[p // n_p * n_out + child][p % n_p, :, q * TILE : (q + 1) * TILE] = view[
                        row_at[child, p] + base, :, pl.ds(lane, TILE)
                    ]

    out = like((n_p, k, n_q * TILE))
    flat = pl.pallas_call(
        kernel,
        out_shape=[out] * (n_out * cuts),
        grid_spec=pltpu.PrefetchScalarGridSpec(
            num_scalar_prefetch=3,
            grid=(1,),
            in_specs=[any_spec()] * n_pieces,
            out_specs=[pl.BlockSpec(out.shape, lambda i, *_: (0, 0, 0))] * (n_out * cuts),
            scratch_shapes=[
                pltpu.VMEM((n_pieces,) + pieces[1].shape, F32),
                pltpu.SemaphoreType.DMA((n_pieces,)),
            ],
        ),
        compiler_params=params(24),
        cost_estimate=cost(),
    )(row_at, col_at, lane_at, *pieces)
    return [flat[i * n_out : (i + 1) * n_out] for i in range(cuts)]


def halves(x):
    hi = x.astype(BF16)
    return hi, (x - hi.astype(F32)).astype(BF16)


def three(ah, al, bh, bl):
    d = lambda a, b: jnp.dot(a, b, preferred_element_type=F32)
    return d(ah, bh) + (d(ah, bl) + d(al, bh))


def split(top, bottom, block=256):
    rows, width = top.shape
    steps = rows // block

    def kernel(a, b, hi, lo):
        i = pl.program_id(0)

        @pl.when(i < steps)
        def _():
            hi[...], lo[...] = halves(a[...])

        @pl.when(i >= steps)
        def _():
            hi[...], lo[...] = halves(b[...])

    out = like((2 * rows, width), BF16)
    return pl.pallas_call(
        kernel,
        out_shape=[out, out],
        grid=(2 * steps,),
        in_specs=[
            pl.BlockSpec((block, width), lambda i: (jnp.minimum(i, steps - 1), 0)),
            pl.BlockSpec((block, width), lambda i: (jnp.maximum(i - steps, 0), 0)),
        ],
        out_specs=[pl.BlockSpec((block, width), lambda i: (i, 0))] * 2,
        compiler_params=params(16),
        cost_estimate=cost(),
    )(top, bottom)


def turn(blocks, shape, col_id, same):
    n_p, n_low, n_col, n_ch, k = shape
    width = blocks[0].shape[1]
    deep = n_p * n_low * k
    views = [b.reshape(n_p, n_low, n_col, n_ch, k, width) for b in blocks]
    flags = jnp.stack([col_id, same.astype(jnp.int32)])
    half_p = n_p // 2
    pieces = [[(core, far, 0, 0, n_p)] for core in range(2) for far in range(n_col)]
    pieces += [[(core, 0, 1, 0, n_p)] for core in range(2)]
    pieces += [[(core, 1, 1, 0, n_p)] for core in range(2)]
    moves = []
    for at, piece in enumerate(pieces):
        row = 0
        for core, far, ch, tile, tiles in piece:
            moves.append((at, row, core, far, ch, tile, tiles))
            row += tiles

    def kernel(flag, own, own_p, far, far_p, hi, lo, buf, sems):
        i = pl.program_id(0)

        @pl.when(i == 0)
        def _():
            for use, refs in ((1, (own, own_p)), (0, (far, far_p))):

                @pl.when(flag[1] == use)
                def _(refs=refs):
                    for at, row, core, side, ch, tile, tiles in moves:
                        pltpu.make_async_copy(
                            refs[core].at[pl.ds(tile, tiles), :, flag[0] ^ side, ch],
                            buf.at[at, pl.ds(row, tiles)],
                            sems.at[at],
                        ).start()

        pltpu.make_async_copy(own.at[:, :, flag[0], 0], buf.at[i], sems.at[i]).wait()
        hi[0], lo[0] = halves(buf[i].reshape(deep, width).T)

    out = like((len(pieces), width, deep), BF16)
    return pl.pallas_call(
        kernel,
        out_shape=[out, out],
        grid_spec=pltpu.PrefetchScalarGridSpec(
            num_scalar_prefetch=1,
            grid=(len(pieces),),
            in_specs=[any_spec()] * 4,
            out_specs=[pl.BlockSpec((1, width, deep), lambda i, *_: (i, 0, 0))] * 2,
            scratch_shapes=[
                pltpu.VMEM((len(pieces), n_p, n_low, k, width), F32),
                pltpu.SemaphoreType.DMA((len(pieces),)),
            ],
        ),
        compiler_params=params(32),
        cost_estimate=cost(),
    )(flags, *views)


def panel(blocks, low_id):
    n_low = len(blocks)
    n_p, k, deep = blocks[0].shape
    rows = n_p * n_low * k

    def kernel(at, *refs):
        ins, (mh, ml, full) = refs[:n_low], refs[n_low:]
        for s in range(n_low):
            full[:, at[0] ^ s] = ins[s][...]
        mh[...], ml[...] = halves(full[...].reshape(rows, -1))

    out = like((rows, deep), BF16)
    wide = deep // 2
    return pl.pallas_call(
        kernel,
        out_shape=[out, out],
        grid_spec=pltpu.PrefetchScalarGridSpec(
            num_scalar_prefetch=1,
            grid=(deep // wide,),
            in_specs=[pl.BlockSpec((n_p, k, wide), lambda i, *_: (0, 0, i))] * n_low,
            out_specs=[pl.BlockSpec((rows, wide), lambda i, *_: (0, i))] * 2,
            scratch_shapes=[pltpu.VMEM((n_p, n_low, k, wide), F32)],
        ),
        compiler_params=params(16),
        cost_estimate=cost(),
    )(low_id.reshape(1), *blocks)


def product(panels, parts, shape, wide=512):
    deep = panels[0][0].shape[1]
    _, n_low, _, _, k = shape
    tiles = [m[0].shape[0] // (n_low * k) for m in panels]
    n_p = sum(tiles)
    rows = n_p * n_low * k
    steps = parts[0][0].shape[1] // wide
    n, n_m = len(parts), len(panels)

    def kernel(*refs):
        out = refs[-1]
        for j in range(n):

            @pl.when(pl.program_id(0) // steps == j)
            def _(j=j):
                hi, lo = refs[2 * n_m + 2 * j : 2 * n_m + 2 * j + 2]
                tile = 0
                for i in range(n_m):
                    mh, ml = refs[2 * i : 2 * i + 2]
                    new = -three(mh[...], ml[...], hi[...], lo[...])
                    out[tile : tile + tiles[i]] = new.reshape(tiles[i], n_low, k, wide)
                    tile += tiles[i]

    out = like((n_p, n_low, k, n * steps * wide))
    specs, args = [], []
    for m in panels:
        specs += [pl.BlockSpec(m[0].shape, lambda i: (0, 0))] * 2
        args += m
    for j, part in enumerate(parts):
        strip = pl.BlockSpec(
            (deep, wide), lambda i, j=j: (0, jnp.clip(i - j * steps, 0, steps - 1))
        )
        specs += [strip, strip]
        args += part
    return pl.pallas_call(
        kernel,
        out_shape=out,
        grid=(n * steps,),
        in_specs=specs,
        out_specs=pl.BlockSpec((n_p, n_low, k, wide), lambda i: (0, 0, 0, i)),
        compiler_params=params(32),
        cost_estimate=cost(),
    )(*args)


def update(base, turned, pieces, in_place, wide=512):
    height, width = base.shape
    n = len(pieces)
    tall = height // 2
    strip = pl.BlockSpec((height, wide), lambda i: (0, i))
    specs, args, plan = [strip], [base], []
    for at, blocks in pieces:
        for part in turned:
            for x in part:
                deep = x.shape[2]
                specs.append(pl.BlockSpec((1, tall, deep), lambda i, at=at: (at, 0, 0)))
                args.append(x)
        for columns in blocks:
            columns = [x if isinstance(x, tuple) else (x, None) for x in columns]
            steps = columns[0][0].shape[-1] // wide
            plan.append((len(blocks), len(columns), steps))
            for j, (x, row) in enumerate(columns):
                x = x.reshape(-1, x.shape[-1])
                specs.append(
                    pl.BlockSpec(
                        (x.shape[0] if row is None else turned[0][0].shape[2], wide),
                        lambda i, j=j, steps=steps, row=row or 0: (
                            row,
                            jnp.clip(i - j * steps, 0, steps - 1),
                        ),
                    )
                )
                args.append(x)
    n_in = len(args)

    def kernel(*refs):
        acc, out = refs[0], refs[n_in]
        where = pl.program_id(0)
        top, bottom = acc[:tall], acc[tall:]
        at, row = 1, 0
        for _ in range(n):
            upper, lower_ = refs[at : at + 2], refs[at + 2 : at + 4]
            at += 4
            rows = []
            for _ in range(plan[row][0]):
                _, columns, steps = plan[row]
                x = refs[at][...]
                for j in range(1, columns):
                    x = jnp.where(where // steps == j, refs[at + j][...], x)
                rows.append(x)
                at += columns
                row += 1
            sh, sl = halves(rows[0] if len(rows) == 1 else jnp.concatenate(rows, axis=0))
            top = top - three(upper[0][0], upper[1][0], sh, sl)
            bottom = bottom - three(lower_[0][0], lower_[1][0], sh, sl)
        out[:tall], out[tall:] = top, bottom

    deep = turned[0][0].shape[2] * n
    return pl.pallas_call(
        kernel,
        out_shape=like(base.shape),
        grid=(width // wide,),
        in_specs=specs,
        out_specs=strip,
        input_output_aliases={0: 0} if in_place else {},
        compiler_params=params(40),
        cost_estimate=cost(),
    )(*args)


def place(pieces, into, shape, col_id, width):
    n_p, n_low, n_col, n_ch, k = shape
    n = len(pieces)

    def kernel(at, *refs):
        ins, out, sems = refs[:n], refs[-2], refs[-1]
        copies = []
        for i, (rows, skip, count, tile, far, ch, start) in enumerate(pieces):
            tiles, cols = pl.ds(tile, count), pl.ds(start, rows.shape[-1])
            spot = out.at[tiles, :, at[0] ^ far, ch, :, cols]
            copies.append(
                pltpu.make_async_copy(ins[i].at[pl.ds(skip, count)], spot, sems.at[i])
            )
        for copy in copies:
            copy.start()
        for copy in copies:
            copy.wait()

    args = [x[0] for x in pieces]
    specs = [pl.BlockSpec(memory_space=pltpu.VMEM)] * n
    aliases = {}
    if into is not None:
        args.append(into)
        specs.append(any_spec())
        aliases = {n + 1: 0}
    return pl.pallas_call(
        kernel,
        out_shape=like((n_p, n_low, n_col, n_ch, k, width)),
        grid_spec=pltpu.PrefetchScalarGridSpec(
            num_scalar_prefetch=1,
            in_specs=specs,
            out_specs=any_spec(),
            scratch_shapes=[pltpu.SemaphoreType.DMA((n,))],
        ),
        input_output_aliases=aliases,
        compiler_params=params(16),
        cost_estimate=cost(),
    )(col_id.reshape(1), *args)


def body(sigma_top, structure, lower, dinv):
    own = lower[0]
    half_id, low_id = lax.axis_index(HALF), lax.axis_index(LOW)
    row_id, col_id = lax.axis_index("row"), lax.axis_index("col")
    n_half, n_low = lax.axis_size(HALF), lax.axis_size(LOW)
    n_row, n_col = lax.axis_size("row"), lax.axis_size("col")
    groups = n_low * n_col
    n_ch = 2
    k = TILE // groups // n_ch
    rt, width = sigma_top.shape[0] // TILE, sigma_top.shape[1]
    n_q = structure.shape[1]
    n_p = n_q // n_row
    near_id = low_id * n_col + col_id

    children = half_id * n_low + (low_id ^ jnp.arange(n_low, dtype=jnp.int32))
    lists = jnp.take(structure, children, axis=0)
    mine = lax.dynamic_slice_in_dim(lists, row_id * n_p, n_p, axis=1)
    other = lax.dynamic_slice_in_dim(lists, (1 - row_id) * n_p, n_p, axis=1)
    cols = jnp.concatenate([mine, other], axis=1)

    parts = sigma_top.reshape(rt, groups, n_ch, k, width)
    got = lax.all_to_all(pack(parts), (LOW, "col"), 0, 0)
    cut = own.shape[1] // 2
    far = [swap(after(own[:, i * cut : (i + 1) * cut], got), "col", 1) for i in range(2)]
    own_p = swap(own, "row", 1)
    merge = max(1, TILE // width)
    if merge > 1:
        got = (
            got.reshape(groups // merge, merge, n_ch, rt, k, width)
            .transpose(0, 2, 3, 4, 1, 5)
            .reshape(groups // merge, n_ch, rt, k, merge * width)
        )
    got_p = swap(got, "row", 1)
    shape = (n_p, n_low, n_col, n_ch, k)

    def others(chunk):
        return [swap(chunk, HALF, s) for s in range(1, n_half)]

    def choose(got, ring, ch, cuts):
        pieces = [got] + ring + [got_p] + [swap(x, "row", 1) for x in ring]
        return select(pieces, ch, mine, cols, row_id, half_id, n_half, cuts)

    def hand_out(chosen):
        return [chosen[0]] + [swap(chosen[s], LOW, s) for s in range(1, n_low)]

    same = row_id == col_id
    own_c = [own[:, i * cut : (i + 1) * cut] for i in range(2)]
    own_pc = [own_p[:, i * cut : (i + 1) * cut] for i in range(2)]
    near = [split(x, y) for x, y in zip(own_c, own_pc)]
    ring = others(got[:, 0])
    ring[-1] = after(ring[-1], near[0][0], near[1][0])
    far[0] = after(far[0], ring[-1])
    far_p = [swap(far[0], "row", 1)]
    (chosen,) = choose(got, ring, 0, 1)
    blocks = hand_out(chosen)
    far_parts = [split(after(far[0], chosen[0]), far_p[0])]
    turned = [turn((own_c[0], own_pc[0], far[0], far_p[0]), shape, col_id, same)]
    ring = others(after(got[:, 1], ring[-1]))
    ring[-1] = after(ring[-1], far_parts[0][0], turned[0][0])
    far[1], *blocks = after_all((far[1], *blocks), ring[-1])
    far_p.append(swap(far[1], "row", 1))
    first = panel(blocks, low_id)
    sent = product([first], far_parts[:1], shape)
    came = [(swap(sent, "col", 1), 0, 0, 0)]
    chosen = choose(after(got, sent), ring, 1, 1)
    units = [hand_out(x) for x in chosen]
    far_parts.append(split(after(far[1], chosen[0][0]), far_p[1]))
    last = product([first], far_parts[1:], shape)
    came.append((swap(last, "col", 1), 0, 0, cut))
    turned.append(
        turn((after(own_c[1], last), own_pc[1], far[1], far_p[1]), shape, col_id, same)
    )
    kept = [[product([after_all(first, turned[1][0])], near, shape)]]
    second = panel(after_all(units[0], kept[0][0], came[0][0], came[1][0]), low_id)
    last = product([second], far_parts, shape)
    came.append((swap(last, "col", 1), 0, 1, 0))
    came_p = [swap(after(came[i][0], last), "row", 1) for i in range(2)]
    second = after_all(second, last)
    kept.append([product([second], [x], shape) for x in near])
    kept_p = [[swap(after(x, last), "row", 1) for x in xs] for xs in kept]

    def other_core(x):
        return swap(x, "row", 1)

    base = n_row * n_col
    front = update(
        dinv[0],
        turned,
        [
            (0, [kept[0]]),
            (n_col, [kept_p[0]]),
            (base, [kept[1]]),
            (base + 1, [kept_p[1]]),
            (1, [[came[0][0], came[1][0]]]),
            (n_col + 1, [came_p]),
        ],
        False,
    )
    end = after(came[2][0], front)
    front = update(
        front, turned, [(base + 2, [[end]]), (base + 3, [[other_core(end)]])], True
    )
    cross = None
    for group in (
        [(kept[ch][i], 0, n_p, 0, 0, ch, i * cut) for ch in range(n_ch) for i in range(len(kept[ch]))]
        + [(r, 0, r.shape[0], t, 1, c, x) for r, t, c, x in came[:2]],
        [(r, 0, r.shape[0], t, 1, c, x) for r, t, c, x in came[2:]],
    ):
        cross = place(group, cross, shape, col_id, own.shape[1])
    return (cross.reshape(own.shape)[None], front[None])


def solution(mesh):
    n_leaf, n_row, n_col = (mesh.shape[a] for a in ("leaf", "row", "col"))
    fine = Mesh(
        mesh.devices.reshape(n_leaf // NEAR, NEAR, n_row, n_col), (HALF, LOW, "row", "col")
    )
    leaf = (HALF, LOW)
    block = P(leaf, "row", "col")
    return jax.shard_map(
        body,
        mesh=fine,
        in_specs=(P("row", leaf + ("col",)), P(), block, block),
        out_specs=(block, block),
        check_vma=False,
    )
```

```python
import jax
import jax.numpy as jnp
from jax import lax
from jax.experimental import pallas as pl
from jax.experimental.pallas import tpu as pltpu
from jax.sharding import Mesh
from jax.sharding import PartitionSpec as P

TILE = 128
NEAR = 4
HALF = "half"
LOW = "low"
F32 = jnp.float32
BF16 = jnp.bfloat16


def swap(x, axis, bit):
    names = axis if isinstance(axis, tuple) else (axis,)
    size = 1
    for name in names:
        size *= lax.axis_size(name)
    return lax.ppermute(x, axis, [(i, i ^ bit) for i in range(size)])


def after(x, *deps):
    return lax.optimization_barrier((x,) + deps)[0]


def after_all(xs, *deps):
    return lax.optimization_barrier(tuple(xs) + deps)[: len(xs)]


def params(mib):
    return pltpu.CompilerParams(vmem_limit_bytes=mib << 20)


def cost():
    return pl.CostEstimate(flops=1, transcendentals=0, bytes_accessed=1)


def any_spec():
    return pl.BlockSpec(memory_space=pl.ANY)


def like(shape, dtype=F32):
    return jax.ShapeDtypeStruct(shape, dtype)


def pack(parts):
    rt, groups, n_ch, k, width = parts.shape

    def kernel(src, out):
        for ch in range(n_ch):
            out[0, ch] = src[:, 0, ch]

    return pl.pallas_call(
        kernel,
        out_shape=like((groups, n_ch, rt, k, width)),
        grid=(groups,),
        in_specs=[pl.BlockSpec((rt, 1, n_ch, k, width), lambda i: (0, i, 0, 0, 0))],
        out_specs=pl.BlockSpec((1, n_ch, rt, k, width), lambda i: (i, 0, 0, 0, 0)),
        compiler_params=params(16),
        cost_estimate=cost(),
    )(parts)


def select(pieces, chunk, rows, cols, row_id, half_id, n_half, cuts):
    n_src, rt, k, width = pieces[1].shape
    n_out, n_q = cols.shape
    n_p = rows.shape[1] // cuts
    per_src = width // TILE
    in_half = n_src * per_src
    n_pieces = len(pieces)
    src = cols % in_half // per_src
    row_at = ((rows // rt) ^ row_id) * (n_half * n_src * rt) + rows % rt
    col_at = ((cols // in_half) ^ half_id) * (n_src * rt) + src * rt
    lane_at = cols % per_src * TILE

    def kernel(row_at, col_at, lane_at, *refs):
        ins, outs = refs[:n_pieces], refs[n_pieces:-2]
        table, sems = refs[-2:]
        copies = []
        for i in range(n_pieces):
            piece = ins[i].at[:, chunk] if i % n_half == 0 else ins[i]
            copies.append(pltpu.make_async_copy(piece, table.at[i], sems.at[i]))
        for copy in copies:
            copy.start()
        for copy in copies:
            copy.wait()
        view = table.reshape(n_pieces * n_src * rt, k, width)
        for child in range(n_out):
            for q in range(n_q):
                base = col_at[child, q]
                lane = pl.multiple_of(lane_at[child, q], TILE)
                for p in range(n_p * cuts):
                    outs[p // n_p * n_out + child][p % n_p, :, q * TILE : (q + 1) * TILE] = view[
                        row_at[child, p] + base, :, pl.ds(lane, TILE)
                    ]

    out = like((n_p, k, n_q * TILE))
    flat = pl.pallas_call(
        kernel,
        out_shape=[out] * (n_out * cuts),
        grid_spec=pltpu.PrefetchScalarGridSpec(
            num_scalar_prefetch=3,
            grid=(1,),
            in_specs=[any_spec()] * n_pieces,
            out_specs=[pl.BlockSpec(out.shape, lambda i, *_: (0, 0, 0))] * (n_out * cuts),
            scratch_shapes=[
                pltpu.VMEM((n_pieces,) + pieces[1].shape, F32),
                pltpu.SemaphoreType.DMA((n_pieces,)),
            ],
        ),
        compiler_params=params(24),
        cost_estimate=cost(),
    )(row_at, col_at, lane_at, *pieces)
    return [flat[i * n_out : (i + 1) * n_out] for i in range(cuts)]


def halves(x):
    hi = x.astype(BF16)
    return hi, (x - hi.astype(F32)).astype(BF16)


def three(ah, al, bh, bl):
    d = lambda a, b: jnp.dot(a, b, preferred_element_type=F32)
    return d(ah, bh) + (d(ah, bl) + d(al, bh))


def split(top, bottom, block=512):
    rows, width = top.shape
    steps = rows // block

    def kernel(a, b, hi, lo):
        i = pl.program_id(0)

        @pl.when(i < steps)
        def _():
            hi[...], lo[...] = halves(a[...])

        @pl.when(i >= steps)
        def _():
            hi[...], lo[...] = halves(b[...])

    out = like((2 * rows, width), BF16)
    return pl.pallas_call(
        kernel,
        out_shape=[out, out],
        grid=(2 * steps,),
        in_specs=[
            pl.BlockSpec((block, width), lambda i: (jnp.minimum(i, steps - 1), 0)),
            pl.BlockSpec((block, width), lambda i: (jnp.maximum(i - steps, 0), 0)),
        ],
        out_specs=[pl.BlockSpec((block, width), lambda i: (i, 0))] * 2,
        compiler_params=params(16),
        cost_estimate=cost(),
    )(top, bottom)


def turn(blocks, shape, col_id, same):
    n_p, n_low, n_col, n_ch, k = shape
    width = blocks[0].shape[1]
    deep = n_p * n_low * k
    views = [b.reshape(n_p, n_low, n_col, n_ch, k, width) for b in blocks]
    flags = jnp.stack([col_id, same.astype(jnp.int32)])
    half_p = n_p // 2
    pieces = [[(core, far, 0, 0, n_p)] for core in range(2) for far in range(n_col)]
    pieces += [[(core, 0, 1, 0, n_p)] for core in range(2)]
    pieces += [[(core, 1, 1, 0, n_p)] for core in range(2)]
    moves = []
    for at, piece in enumerate(pieces):
        row = 0
        for core, far, ch, tile, tiles in piece:
            moves.append((at, row, core, far, ch, tile, tiles))
            row += tiles

    def kernel(flag, own, own_p, far, far_p, hi, lo, buf, sems):
        i = pl.program_id(0)

        @pl.when(i == 0)
        def _():
            for use, refs in ((1, (own, own_p)), (0, (far, far_p))):

                @pl.when(flag[1] == use)
                def _(refs=refs):
                    for at, row, core, side, ch, tile, tiles in moves:
                        pltpu.make_async_copy(
                            refs[core].at[pl.ds(tile, tiles), :, flag[0] ^ side, ch],
                            buf.at[at, pl.ds(row, tiles)],
                            sems.at[at],
                        ).start()

        pltpu.make_async_copy(own.at[:, :, flag[0], 0], buf.at[i], sems.at[i]).wait()
        hi[0], lo[0] = halves(buf[i].reshape(deep, width).T)

    out = like((len(pieces), width, deep), BF16)
    return pl.pallas_call(
        kernel,
        out_shape=[out, out],
        grid_spec=pltpu.PrefetchScalarGridSpec(
            num_scalar_prefetch=1,
            grid=(len(pieces),),
            in_specs=[any_spec()] * 4,
            out_specs=[pl.BlockSpec((1, width, deep), lambda i, *_: (i, 0, 0))] * 2,
            scratch_shapes=[
                pltpu.VMEM((len(pieces), n_p, n_low, k, width), F32),
                pltpu.SemaphoreType.DMA((len(pieces),)),
            ],
        ),
        compiler_params=params(32),
        cost_estimate=cost(),
    )(flags, *views)


def panel(blocks, low_id):
    n_low = len(blocks)
    n_p, k, deep = blocks[0].shape
    rows = n_p * n_low * k

    def kernel(at, *refs):
        ins, (mh, ml, full) = refs[:n_low], refs[n_low:]
        for s in range(n_low):
            full[:, at[0] ^ s] = ins[s][...]
        mh[...], ml[...] = halves(full[...].reshape(rows, -1))

    out = like((rows, deep), BF16)
    wide = deep
    return pl.pallas_call(
        kernel,
        out_shape=[out, out],
        grid_spec=pltpu.PrefetchScalarGridSpec(
            num_scalar_prefetch=1,
            grid=(deep // wide,),
            in_specs=[pl.BlockSpec((n_p, k, wide), lambda i, *_: (0, 0, i))] * n_low,
            out_specs=[pl.BlockSpec((rows, wide), lambda i, *_: (0, i))] * 2,
            scratch_shapes=[pltpu.VMEM((n_p, n_low, k, wide), F32)],
        ),
        compiler_params=params(16),
        cost_estimate=cost(),
    )(low_id.reshape(1), *blocks)


def product(panels, parts, shape, wide=512):
    deep = panels[0][0].shape[1]
    _, n_low, _, _, k = shape
    tiles = [m[0].shape[0] // (n_low * k) for m in panels]
    n_p = sum(tiles)
    rows = n_p * n_low * k
    steps = parts[0][0].shape[1] // wide
    n, n_m = len(parts), len(panels)

    def kernel(*refs):
        out = refs[-1]
        for j in range(n):

            @pl.when(pl.program_id(0) // steps == j)
            def _(j=j):
                hi, lo = refs[2 * n_m + 2 * j : 2 * n_m + 2 * j + 2]
                tile = 0
                for i in range(n_m):
                    mh, ml = refs[2 * i : 2 * i + 2]
                    new = -three(mh[...], ml[...], hi[...], lo[...])
                    out[tile : tile + tiles[i]] = new.reshape(tiles[i], n_low, k, wide)
                    tile += tiles[i]

    out = like((n_p, n_low, k, n * steps * wide))
    specs, args = [], []
    for m in panels:
        specs += [pl.BlockSpec(m[0].shape, lambda i: (0, 0))] * 2
        args += m
    for j, part in enumerate(parts):
        strip = pl.BlockSpec(
            (deep, wide), lambda i, j=j: (0, jnp.clip(i - j * steps, 0, steps - 1))
        )
        specs += [strip, strip]
        args += part
    return pl.pallas_call(
        kernel,
        out_shape=out,
        grid=(n * steps,),
        in_specs=specs,
        out_specs=pl.BlockSpec((n_p, n_low, k, wide), lambda i: (0, 0, 0, i)),
        compiler_params=params(32),
        cost_estimate=cost(),
    )(*args)


def update(base, turned, pieces, in_place, wide=512):
    height, width = base.shape
    n = len(pieces)
    tall = height // 2
    strip = pl.BlockSpec((height, wide), lambda i: (0, i))
    specs, args, plan = [strip], [base], []
    for at, blocks in pieces:
        for part in turned:
            for x in part:
                deep = x.shape[2]
                specs.append(pl.BlockSpec((1, tall, deep), lambda i, at=at: (at, 0, 0)))
                args.append(x)
        for columns in blocks:
            columns = [x if isinstance(x, tuple) else (x, None) for x in columns]
            steps = columns[0][0].shape[-1] // wide
            plan.append((len(blocks), len(columns), steps))
            for j, (x, row) in enumerate(columns):
                x = x.reshape(-1, x.shape[-1])
                specs.append(
                    pl.BlockSpec(
                        (x.shape[0] if row is None else turned[0][0].shape[2], wide),
                        lambda i, j=j, steps=steps, row=row or 0: (
                            row,
                            jnp.clip(i - j * steps, 0, steps - 1),
                        ),
                    )
                )
                args.append(x)
    n_in = len(args)

    def kernel(*refs):
        acc, out = refs[0], refs[n_in]
        where = pl.program_id(0)
        top, bottom = acc[:tall], acc[tall:]
        at, row = 1, 0
        for _ in range(n):
            upper, lower_ = refs[at : at + 2], refs[at + 2 : at + 4]
            at += 4
            rows = []
            for _ in range(plan[row][0]):
                _, columns, steps = plan[row]
                x = refs[at][...]
                for j in range(1, columns):
                    x = jnp.where(where // steps == j, refs[at + j][...], x)
                rows.append(x)
                at += columns
                row += 1
            sh, sl = halves(rows[0] if len(rows) == 1 else jnp.concatenate(rows, axis=0))
            top = top - three(upper[0][0], upper[1][0], sh, sl)
            bottom = bottom - three(lower_[0][0], lower_[1][0], sh, sl)
        out[:tall], out[tall:] = top, bottom

    deep = turned[0][0].shape[2] * n
    return pl.pallas_call(
        kernel,
        out_shape=like(base.shape),
        grid=(width // wide,),
        in_specs=specs,
        out_specs=strip,
        input_output_aliases={0: 0} if in_place else {},
        compiler_params=params(40),
        cost_estimate=cost(),
    )(*args)


def place(pieces, into, shape, col_id, width):
    n_p, n_low, n_col, n_ch, k = shape
    n = len(pieces)

    def kernel(at, *refs):
        ins, out, sems = refs[:n], refs[-2], refs[-1]
        copies = []
        for i, (rows, skip, count, tile, far, ch, start) in enumerate(pieces):
            tiles, cols = pl.ds(tile, count), pl.ds(start, rows.shape[-1])
            spot = out.at[tiles, :, at[0] ^ far, ch, :, cols]
            copies.append(
                pltpu.make_async_copy(ins[i].at[pl.ds(skip, count)], spot, sems.at[i])
            )
        for copy in copies:
            copy.start()
        for copy in copies:
            copy.wait()

    args = [x[0] for x in pieces]
    specs = [pl.BlockSpec(memory_space=pltpu.VMEM)] * n
    aliases = {}
    if into is not None:
        args.append(into)
        specs.append(any_spec())
        aliases = {n + 1: 0}
    return pl.pallas_call(
        kernel,
        out_shape=like((n_p, n_low, n_col, n_ch, k, width)),
        grid_spec=pltpu.PrefetchScalarGridSpec(
            num_scalar_prefetch=1,
            in_specs=specs,
            out_specs=any_spec(),
            scratch_shapes=[pltpu.SemaphoreType.DMA((n,))],
        ),
        input_output_aliases=aliases,
        compiler_params=params(16),
        cost_estimate=cost(),
    )(col_id.reshape(1), *args)


def body(sigma_top, structure, lower, dinv):
    own = lower[0]
    half_id, low_id = lax.axis_index(HALF), lax.axis_index(LOW)
    row_id, col_id = lax.axis_index("row"), lax.axis_index("col")
    n_half, n_low = lax.axis_size(HALF), lax.axis_size(LOW)
    n_row, n_col = lax.axis_size("row"), lax.axis_size("col")
    groups = n_low * n_col
    n_ch = 2
    k = TILE // groups // n_ch
    rt, width = sigma_top.shape[0] // TILE, sigma_top.shape[1]
    n_q = structure.shape[1]
    n_p = n_q // n_row
    near_id = low_id * n_col + col_id

    children = half_id * n_low + (low_id ^ jnp.arange(n_low, dtype=jnp.int32))
    lists = jnp.take(structure, children, axis=0)
    mine = lax.dynamic_slice_in_dim(lists, row_id * n_p, n_p, axis=1)
    other = lax.dynamic_slice_in_dim(lists, (1 - row_id) * n_p, n_p, axis=1)
    cols = jnp.concatenate([mine, other], axis=1)

    parts = sigma_top.reshape(rt, groups, n_ch, k, width)
    got = lax.all_to_all(pack(parts), (LOW, "col"), 0, 0)
    cut = own.shape[1] // 2
    far = [swap(after(own[:, i * cut : (i + 1) * cut], got), "col", 1) for i in range(2)]
    own_p = swap(own, "row", 1)
    merge = max(1, TILE // width)
    if merge > 1:
        got = (
            got.reshape(groups // merge, merge, n_ch, rt, k, width)
            .transpose(0, 2, 3, 4, 1, 5)
            .reshape(groups // merge, n_ch, rt, k, merge * width)
        )
    got_p = swap(got, "row", 1)
    shape = (n_p, n_low, n_col, n_ch, k)

    def others(chunk):
        return [swap(chunk, HALF, s) for s in range(1, n_half)]

    def choose(got, ring, ch, cuts):
        pieces = [got] + ring + [got_p] + [swap(x, "row", 1) for x in ring]
        return select(pieces, ch, mine, cols, row_id, half_id, n_half, cuts)

    def hand_out(chosen):
        return [chosen[0]] + [swap(chosen[s], LOW, s) for s in range(1, n_low)]

    same = row_id == col_id
    own_c = [own[:, i * cut : (i + 1) * cut] for i in range(2)]
    own_pc = [own_p[:, i * cut : (i + 1) * cut] for i in range(2)]
    near = [split(x, y) for x, y in zip(own_c, own_pc)]
    ring = others(got[:, 0])
    ring[-1] = after(ring[-1], near[0][0], near[1][0])
    far[0] = after(far[0], ring[-1])
    far_p = [swap(far[0], "row", 1)]
    (chosen,) = choose(got, ring, 0, 1)
    blocks = hand_out(chosen)
    far_parts = [split(after(far[0], chosen[0]), far_p[0])]
    turned = [turn((own_c[0], own_pc[0], far[0], far_p[0]), shape, col_id, same)]
    ring = others(after(got[:, 1], ring[-1]))
    ring[-1] = after(ring[-1], far_parts[0][0], turned[0][0])
    far[1], *blocks = after_all((far[1], *blocks), ring[-1])
    far_p.append(swap(far[1], "row", 1))
    first = panel(blocks, low_id)
    sent = product([first], far_parts[:1], shape)
    came = [(swap(sent, "col", 1), 0, 0, 0)]
    chosen = choose(after(got, sent), ring, 1, 1)
    units = [hand_out(x) for x in chosen]
    far_parts.append(split(after(far[1], chosen[0][0]), far_p[1]))
    last = product([first], far_parts[1:], shape)
    came.append((swap(last, "col", 1), 0, 0, cut))
    turned.append(
        turn((after(own_c[1], last), own_pc[1], far[1], far_p[1]), shape, col_id, same)
    )
    kept = [[product([after_all(first, turned[1][0])], near, shape)]]
    second = panel(after_all(units[0], kept[0][0], came[0][0], came[1][0]), low_id)
    last = product([second], far_parts, shape)
    came.append((swap(last, "col", 1), 0, 1, 0))
    came_p = [swap(after(came[i][0], last), "row", 1) for i in range(2)]
    second = after_all(second, last)
    kept.append([product([second], [x], shape) for x in near])
    kept_p = [[swap(after(x, last), "row", 1) for x in xs] for xs in kept]

    def other_core(x):
        return swap(x, "row", 1)

    base = n_row * n_col
    front = update(
        dinv[0],
        turned,
        [
            (0, [kept[0]]),
            (n_col, [kept_p[0]]),
            (base, [kept[1]]),
            (base + 1, [kept_p[1]]),
            (1, [[came[0][0], came[1][0]]]),
            (n_col + 1, [came_p]),
        ],
        False,
    )
    end = after(came[2][0], front)
    front = update(
        front, turned, [(base + 2, [[end]]), (base + 3, [[other_core(end)]])], True
    )
    cross = None
    for group in (
        [(kept[ch][i], 0, n_p, 0, 0, ch, i * cut) for ch in range(n_ch) for i in range(len(kept[ch]))]
        + [(r, 0, r.shape[0], t, 1, c, x) for r, t, c, x in came[:2]],
        [(r, 0, r.shape[0], t, 1, c, x) for r, t, c, x in came[2:]],
    ):
        cross = place(group, cross, shape, col_id, own.shape[1])
    return (cross.reshape(own.shape)[None], front[None])


def solution(mesh):
    n_leaf, n_row, n_col = (mesh.shape[a] for a in ("leaf", "row", "col"))
    fine = Mesh(
        mesh.devices.reshape(n_leaf // NEAR, NEAR, n_row, n_col), (HALF, LOW, "row", "col")
    )
    leaf = (HALF, LOW)
    block = P(leaf, "row", "col")
    return jax.shard_map(
        body,
        mesh=fine,
        in_specs=(P("row", leaf + ("col",)), P(), block, block),
        out_specs=(block, block),
        check_vma=False,
    )
```
